256 devices in a mesh: ctx: 32 (over y, z), tp: 8 (over x, core).
Axes of the slice: x: 4, y: 4, z: 8, core: 2. Of those that a mesh axis runs over, the one named last changes fastest.
Arguments:
- ssm_inputs: bfloat16 [8192, 8192], P('ctx', 'tp'), may hold values from -4 to 4
- state_maps: bfloat16 [8192, 8, 256], P('ctx', 'tp'), may hold values from -4 to 4
- ssm_gates: bfloat16 [8192, 8192], P('ctx', 'tp'), may hold values from -4 to 4
- time_steps: float32 [128, 8192], P('tp', 'ctx'), may hold values from -5 to 512
- log_rates: float32 [128], P('tp'), may hold values from -12 to 1
- skip_gain: float32 [128], P('tp'), may hold values from 0.5 to 2
- conv_inputs: bfloat16 [4, 8192], P(None, 'tp'), may hold values from -3 to 3
- conv_maps: bfloat16 [4, 8, 256], P(None, 'tp'), may hold values from -3 to 3
- norm_gain: float32 [8192], P('tp'), may hold values from 0.1 to 1.9
- out_weight: bfloat16 [8192, 4096], P('tp'), may hold values from -0.0625 to 0.0625
- queries: bfloat16 [8192, 8192], P('ctx', 'tp'), may hold values from -5 to 5
- attention_keys: bfloat16 [8192, 1024], P('ctx', 'tp'), may hold values from -5 to 5
- values: bfloat16 [8192, 1024], P('ctx', 'tp'), may hold values from -4 to 4
Outputs:
- ssm_out: bfloat16 [8192, 4096], P(('ctx', 'tp'))
- attn_out: bfloat16 [8192, 8192], P('ctx', 'tp')
The draws below stay inside these ranges and needn't reach their ends.
All inputs are finite; a program needn't handle non-finite values.
Results may differ from the reference program's by a relative error of at most 0.03.
Values may be sent and summed in bfloat16 or wider, within the bound.
No kernel may reach another device: no remote copies, remote signals or barrier semaphores. Data moves between devices by JAX's collectives and lax.ppermute only.
A program may use at most 128 MiB of HBM per device.

```python
import math
import jax
import jax.numpy as jnp
from jax import lax

SPACE_HEADS = 128
SSM_DIM = 64
NSTATE = 128
GROUPS = 8
QUERY_HEADS = 64
KEY_VALUE_HEADS = 8
HEAD_SIZE = 128
DOUT = 4096
CONV = 4
TOK_DEV = 256
TOKEN_COUNT = 8192
N_TP = 8


def simple_jitter(key, shape):
    return jnp.clip(jax.random.normal(key, shape, jnp.float32), -4.0, 4.0)


def space_model_rule(key):
    slow_share = 0.5
    sluggish_heads = jax.random.uniform(jax.random.fold_in(key, 11), (SPACE_HEADS,), jnp.float32) < slow_share
    keep_share = jnp.exp(jax.random.uniform(jax.random.fold_in(key, 12), (SPACE_HEADS,), jnp.float32, math.log(0.2), math.log(0.8)))
    forget = jax.random.uniform(jax.random.fold_in(key, 13), (SPACE_HEADS,), jnp.float32, 30.0, 50.0)
    decline_rate = jnp.where(sluggish_heads, keep_share / (TOKEN_COUNT * 0.02), 1.0 / (forget * 0.02))
    spike_position = jax.random.randint(jax.random.fold_in(key, 14), (3,), 0, TOKEN_COUNT)
    spike_loss = jax.random.uniform(jax.random.fold_in(key, 15), (3, SPACE_HEADS), jnp.float32, 0.2, 0.4)
    return (sluggish_heads, decline_rate, spike_position, spike_loss)


def draw_log_rates(key, part):
    sluggish_heads, decline_rate, spike_position, spike_loss = space_model_rule(key)
    return jnp.log(decline_rate).astype(jnp.float32)


def draw_time_steps(key, part):
    sluggish_heads, decline_rate, spike_position, spike_loss = space_model_rule(key)
    base_step = jnp.exp(jax.random.uniform(jax.random.fold_in(key, 16), (SPACE_HEADS, TOKEN_COUNT), jnp.float32, math.log(0.01), math.log(0.04)))
    token_location = jnp.arange(TOKEN_COUNT)
    flagged = token_location[None, :] == spike_position[:, None]
    spike_step = -jnp.log1p(-spike_loss) / decline_rate[None, :]
    additional_step = jnp.sum(jnp.where(flagged[:, None, :], spike_step[:, :, None], 0.0), axis=0)
    any_flagged = jnp.any(flagged, axis=0)
    step_size = jnp.where(sluggish_heads[:, None] & any_flagged[None, :], additional_step, base_step)
    return (step_size + jnp.log(-jnp.expm1(-step_size))).astype(jnp.float32)


def draw_state_maps(key, part):
    sluggish_heads, decline_rate, spike_position, spike_loss = space_model_rule(key)
    random_jitter = simple_jitter(jax.random.fold_in(key, 17), (TOKEN_COUNT, GROUPS, 2 * NSTATE))
    token_location = jnp.arange(TOKEN_COUNT)
    any_flagged = jnp.any(token_location[None, :] == spike_position[:, None], axis=0)
    b_columns = jnp.arange(2 * NSTATE) < NSTATE
    shrink = jnp.where(any_flagged[:, None, None] & b_columns[None, None, :], 0.0001, 1.0)
    return (random_jitter * shrink).astype(jnp.bfloat16)


def draw_queries(key, part):
    random_jitter = simple_jitter(jax.random.fold_in(key, 1), (TOKEN_COUNT, QUERY_HEADS * HEAD_SIZE))
    return random_jitter.astype(jnp.bfloat16)


def draw_attention_keys(key, part):
    random_jitter = simple_jitter(jax.random.fold_in(key, 2), (TOKEN_COUNT, KEY_VALUE_HEADS * HEAD_SIZE))
    return random_jitter.astype(jnp.bfloat16)


def block_levels(stream_key, shape, shards, low, largest):
    level = 1.0
    for axis_at, shards_of in shards:
        heights = jax.random.uniform(jax.random.fold_in(jax.random.fold_in(stream_key, 6), axis_at), (shards_of,), jnp.float32, low / len(shards), largest / len(shards))
        level = level * jnp.repeat(jnp.exp(heights), shape[axis_at] // shards_of).reshape((-1,) + (1,) * (len(shape) - 1 - axis_at))
    return level


def bell_draw(stream_key, extent, spread, limit, cuts=(), kind=jnp.bfloat16):
    loudness = block_levels(stream_key, extent, cuts, -0.22, 0.18) if cuts else 1.0
    values = jax.random.normal(stream_key, extent, jnp.float32) * spread * loudness
    return jnp.minimum(jnp.maximum(values, -limit), limit).astype(kind)


def setup_inputs(seed: int = 0) -> dict:
    key_list = jax.random.split(jax.random.key(seed), 14)
    ssm_inputs = bell_draw(key_list[0], (TOKEN_COUNT, SPACE_HEADS * SSM_DIM), 1.0, 4.0, ((0, 32), (1, 8)))
    state_maps = draw_state_maps(jax.random.fold_in(key_list[13], 71), 0)
    ssm_gates = bell_draw(key_list[2], (TOKEN_COUNT, SPACE_HEADS * SSM_DIM), 1.0, 4.0, ((0, 32), (1, 8)))
    time_steps = draw_time_steps(jax.random.fold_in(key_list[13], 71), 0)
    log_rates = draw_log_rates(jax.random.fold_in(key_list[13], 71), 0)
    skip_gain = jnp.clip(0.5 + 1.5 * jax.random.uniform(key_list[5], (SPACE_HEADS,), jnp.float32) ** block_levels(key_list[5], (SPACE_HEADS,), ((0, 8),), -0.2, 0.2), 0.5, 2.0)
    conv_inputs = bell_draw(key_list[6], (CONV, SPACE_HEADS * SSM_DIM), CONV ** -0.5, 3.0, ((1, 8),))
    conv_maps = bell_draw(key_list[7], (CONV, GROUPS, 2 * NSTATE), CONV ** -0.5, 3.0, ((1, 8),))
    norm_gain = jnp.clip(1.0 + 0.18 * jax.random.normal(key_list[8], (SPACE_HEADS * SSM_DIM,), jnp.float32), 0.1, 1.9)
    out_weight = bell_draw(key_list[9], (SPACE_HEADS * SSM_DIM, DOUT), (SPACE_HEADS * SSM_DIM) ** -0.5, 0.0625, ((0, 8),))
    queries = draw_queries(jax.random.fold_in(key_list[13], 71), 0)
    attention_keys = draw_attention_keys(jax.random.fold_in(key_list[13], 71), 0)
    values = bell_draw(key_list[12], (TOKEN_COUNT, KEY_VALUE_HEADS * HEAD_SIZE), 1.0, 4.0, ((0, 32), (1, 8)))
    return {"ssm_inputs": ssm_inputs, "state_maps": state_maps, "ssm_gates": ssm_gates, "time_steps": time_steps, "log_rates": log_rates, "skip_gain": skip_gain, "conv_inputs": conv_inputs, "conv_maps": conv_maps, "norm_gain": norm_gain, "out_weight": out_weight, "queries": queries, "attention_keys": attention_keys, "values": values}


def conv_silu(series, conv_taps):
    tap_count = conv_taps.shape[0]
    length = series.shape[0]
    padded = jnp.concatenate([jnp.zeros((tap_count - 1,) + series.shape[1:], series.dtype), series], axis=0)
    summed = jnp.zeros(series.shape, jnp.float32)
    for tap_index in range(tap_count):
        summed = summed + conv_taps[tap_index].astype(jnp.float32) * padded[tap_index:tap_index + length].astype(jnp.float32)
    return lax.optimization_barrier(jax.nn.silu(summed).astype(jnp.bfloat16))

def mix_block(inputs_block, b_block, c_block, steps_block, decline_rate):
    tok_rows = inputs_block.shape[0]
    running_log = jnp.cumsum(steps_block * decline_rate[:, :, None], axis=2)
    map_products = jnp.einsum('tgn,sgn->gts', c_block.astype(jnp.float32), b_block.astype(jnp.float32))
    token_location = jnp.arange(tok_rows).astype(jnp.int32)
    causal = token_location[:, None] >= token_location[None, :]
    log_gap = running_log[:, :, :, None] - running_log[:, :, None, :]
    decay_table = jnp.where(causal, jnp.exp(jnp.minimum(log_gap, 0.0)), 0.0)
    mixer = lax.optimization_barrier((map_products[:, None] * decay_table * steps_block[:, :, None, :]).astype(jnp.bfloat16))
    inputs_float = inputs_block.astype(jnp.float32)
    inner_part = jnp.einsum('gjts,sgjp->tgjp', mixer.astype(jnp.float32), inputs_float)
    tail_weight = jnp.exp(running_log[:, :, -1:] - running_log) * steps_block
    weighted = lax.optimization_barrier((jnp.transpose(tail_weight, (2, 0, 1))[..., None] * inputs_float).astype(jnp.bfloat16))
    block_state = jnp.einsum('sgjp,sgn->gjpn', weighted.astype(jnp.float32), b_block.astype(jnp.float32))
    return (inner_part, block_state, running_log)

def attend(queries, attention_keys, values):
    shared_heads = QUERY_HEADS // KEY_VALUE_HEADS
    query_tile_block = min(512, TOKEN_COUNT)
    block_count = TOKEN_COUNT // query_tile_block
    score_scale = 1.0 / math.sqrt(HEAD_SIZE)
    pieces = []
    for current_block_index in range(block_count):
        upper_limit = (current_block_index + 1) * query_tile_block
        query_row_set = queries[current_block_index * query_tile_block:upper_limit].reshape(query_tile_block, KEY_VALUE_HEADS, shared_heads, HEAD_SIZE)
        key_head_rows = attention_keys[:upper_limit].reshape(upper_limit, KEY_VALUE_HEADS, HEAD_SIZE)
        value_head_rows = values[:upper_limit].reshape(upper_limit, KEY_VALUE_HEADS, HEAD_SIZE)
        query_pos = (current_block_index * query_tile_block + jnp.arange(query_tile_block)).astype(jnp.int32)
        key_pos = jnp.arange(upper_limit).astype(jnp.int32)
        allowed = key_pos[None, :] <= query_pos[:, None]

        def single_head(head_index):
            head_queries = lax.dynamic_index_in_dim(query_row_set, head_index, 1, keepdims=False)
            head_keys = lax.dynamic_index_in_dim(key_head_rows, head_index, 1, keepdims=False)
            head_values = lax.dynamic_index_in_dim(value_head_rows, head_index, 1, keepdims=False)
            scores = jnp.einsum('qrd,kd->rqk', head_queries.astype(jnp.float32), head_keys.astype(jnp.float32)) * score_scale
            scores = jnp.where(allowed[None], scores, -jnp.inf)
            row_peak = lax.optimization_barrier(jnp.max(scores, axis=2, keepdims=True))
            raised = jnp.exp(scores - row_peak)
            row_total = lax.optimization_barrier(jnp.sum(raised, axis=2))
            rounded = lax.optimization_barrier(raised.astype(jnp.bfloat16))
            summed = jnp.einsum('rqk,kd->qrd', rounded.astype(jnp.float32), head_values.astype(jnp.float32))
            return (summed / jnp.transpose(row_total)[..., None]).astype(jnp.bfloat16)
        head_outputs = lax.map(single_head, jnp.arange(KEY_VALUE_HEADS).astype(jnp.int32))
        pieces.append(jnp.transpose(head_outputs, (1, 0, 2, 3)).reshape(query_tile_block, QUERY_HEADS * HEAD_SIZE))
    return jnp.concatenate(pieces, axis=0)

def reference(ssm_inputs, state_maps, ssm_gates, time_steps, log_rates, skip_gain, conv_inputs, conv_maps, norm_gain, out_weight, queries, attention_keys, values):
    per_group = SPACE_HEADS // GROUPS
    block_count = TOKEN_COUNT // TOK_DEV
    mixed_inputs = conv_silu(ssm_inputs, conv_inputs).reshape(block_count, TOK_DEV, GROUPS, per_group, SSM_DIM)
    mixed_maps = conv_silu(state_maps, conv_maps).reshape(block_count, TOK_DEV, GROUPS, 2 * NSTATE)
    b_blocks = mixed_maps[..., :NSTATE]
    c_blocks = mixed_maps[..., NSTATE:]
    step_sizes = jnp.transpose(jax.nn.softplus(time_steps).reshape(GROUPS, per_group, block_count, TOK_DEV), (2, 0, 1, 3))
    decline_rate = -jnp.exp(log_rates).reshape(GROUPS, per_group)
    skip_part = skip_gain.reshape(GROUPS, per_group)[None, :, :, None]

    def advance(entering, blocks):
        inputs_block, b_block, c_block, steps_block = blocks
        inner_part, block_state, running_log = mix_block(inputs_block, b_block, c_block, steps_block, decline_rate)
        carried = jnp.einsum('tgn,gjpn->tgjp', c_block.astype(jnp.float32), entering, precision=lax.Precision.HIGHEST)
        outside = jnp.transpose(jnp.exp(running_log), (2, 0, 1))[..., None] * carried
        ssm_output = inner_part + outside + skip_part * inputs_block.astype(jnp.float32)
        leaving = jnp.exp(running_log[:, :, -1])[:, :, None, None] * entering + block_state
        return (leaving, ssm_output)
    start_state = jnp.zeros((GROUPS, per_group, SSM_DIM, NSTATE), jnp.float32)
    final_state, ssm_output = lax.scan(advance, start_state, (mixed_inputs, b_blocks, c_blocks, step_sizes))
    channel_count = per_group * SSM_DIM
    gated = ssm_output.reshape(TOKEN_COUNT, GROUPS, channel_count) * jax.nn.silu(ssm_gates.reshape(TOKEN_COUNT, GROUPS, channel_count).astype(jnp.float32))
    mean_square = lax.optimization_barrier(jnp.mean(gated * gated, axis=2, keepdims=True))
    normed = ((gated * lax.rsqrt(mean_square + 1e-05)).reshape(TOKEN_COUNT, SPACE_HEADS * SSM_DIM) * norm_gain).astype(jnp.bfloat16)
    slice_rows = SPACE_HEADS * SSM_DIM // N_TP
    ssm_sum = jnp.zeros((TOKEN_COUNT, DOUT), jnp.float32)
    for member in range(N_TP):
        partial_term = jnp.dot(normed[:, member * slice_rows:(member + 1) * slice_rows], out_weight[member * slice_rows:(member + 1) * slice_rows], preferred_element_type=jnp.float32)
        ssm_sum = ssm_sum + lax.optimization_barrier(partial_term.astype(jnp.bfloat16)).astype(jnp.float32)
    ssm_out = ssm_sum.astype(jnp.bfloat16)
    attn_out = attend(queries, attention_keys, values)
    return (ssm_out, attn_out)
```

```python
import functools

import jax
import jax.numpy as jnp
from jax import lax
from jax.experimental import pallas as pl
from jax.experimental.pallas import tpu as pltpu
from jax.sharding import PartitionSpec as P

F32 = jnp.float32
BF16 = jnp.bfloat16

TOK = 256
CH = 1024
HEADS = 16
NS = 128
NY, NZ = 4, 8
NX, NC = 4, 2
PART = 32
PACK = 48
QH = 8
HD = 128
DOUT = 4096
LOG2E = 1.4426950408889634


def dot_tt(a, b):
    return lax.dot_general(a, b, (((1,), (1,)), ((), ())), preferred_element_type=F32)


def lane_pair(lane, left, right):
    return jnp.where(lane < 64, left, right)


def sigmoid(x):
    return 1.0 / (1.0 + jnp.exp(-x))


def local_kernel(halo, xs, maps, taps_x, taps_m, steps, rates, pack, xc, bc, cols, rows, ext):
    ext[0:8, :] = halo[...].astype(F32)
    ext[8 : 8 + TOK, 0:CH] = xs[...].astype(F32)
    ext[8 : 8 + TOK, CH : CH + 256] = maps[...].astype(F32)
    weights_x = taps_x[...].astype(F32)
    weights_m = taps_m[...].astype(F32)

    def conv(lo, width, w):
        total = w[0:1] * ext[5 : 5 + TOK, lo : lo + width]
        for k in range(1, 4):
            total = total + w[k : k + 1] * ext[5 + k : 5 + k + TOK, lo : lo + width]
        return (total * sigmoid(total)).astype(BF16)

    bc[...] = conv(CH, 256, weights_m)
    dt = jax.nn.softplus(steps[...])
    eye = lax.broadcasted_iota(jnp.int32, (HEADS, HEADS), 0) == lax.broadcasted_iota(
        jnp.int32, (HEADS, HEADS), 1
    )
    rate_row = -jnp.exp(rates[...])
    rate = jnp.sum(
        jnp.where(eye, jnp.broadcast_to(rate_row, (HEADS, HEADS)), 0.0), axis=1, keepdims=True
    )
    cum = dt * rate
    token = lax.broadcasted_iota(jnp.int32, (HEADS, TOK), 1)
    for s in (1, 2, 4, 8, 16, 32, 64, 128):
        cum = cum + jnp.where(token >= s, pltpu.roll(cum, s, 1), 0.0)
    total = cum[:, TOK - 1 : TOK]
    tail = jnp.exp(total - cum) * dt
    rows[0:HEADS, :] = cum
    rows[HEADS : 2 * HEADS, :] = dt
    stacked = jnp.concatenate(
        [tail, cum, jnp.exp(cum), jnp.zeros((128 - 3 * HEADS, TOK), F32)], axis=0
    )
    columns = jnp.transpose(stacked)
    cols[...] = columns
    lane = lax.broadcasted_iota(jnp.int32, (TOK, 128), 1)
    b = bc[:, 0:NS]
    for j in range(8):
        lo = 128 * j
        x = conv(lo, 128, weights_x[:, lo : lo + 128])
        xc[:, lo : lo + 128] = x
        tail_pair = lane_pair(lane, columns[:, 2 * j : 2 * j + 1], columns[:, 2 * j + 1 : 2 * j + 2])
        weighted = (tail_pair * x.astype(F32)).astype(BF16)
        state = lax.dot_general(
            weighted, b, (((0,), (0,)), ((), ())), preferred_element_type=F32
        )
        pack[4 * j : 4 * j + 4, 0:PART, :] = state.astype(BF16).reshape(4, PART, NS)
    row = lax.broadcasted_iota(jnp.int32, (PACK - PART, NS), 0)
    hi = total.astype(BF16).astype(F32)
    mid = (total - hi).astype(BF16).astype(F32)
    low = total - hi - mid
    for h in range(HEADS):
        piece = jnp.where(
            row == 0,
            hi[h : h + 1, :],
            jnp.where(row == 1, mid[h : h + 1, :], jnp.where(row == 2, low[h : h + 1, :], 0.0)),
        ).astype(BF16)
        pack[2 * h, PART:PACK, :] = piece
        pack[2 * h + 1, PART:PACK, :] = piece


def local_part(halo, xs, maps, taps_x, taps_m, steps, rates):
    return pl.pallas_call(
        local_kernel,
        out_shape=(
            jax.ShapeDtypeStruct((32, PACK, NS), BF16),
            jax.ShapeDtypeStruct((TOK, CH), BF16),
            jax.ShapeDtypeStruct((TOK, 256), BF16),
            jax.ShapeDtypeStruct((TOK, 128), F32),
            jax.ShapeDtypeStruct((2 * HEADS, TOK), F32),
        ),
        scratch_shapes=[pltpu.VMEM((TOK + 8, CH + 256), F32)],
        name="mixer_local",
    )(halo, xs, maps, taps_x, taps_m, steps, rates)


def scan_kernel(got, out):
    entering = jnp.zeros((PART, NS), F32)
    for b in range(NY * NZ):
        out[b] = entering.astype(BF16)
        block = got[b].astype(F32)
        log_decay = block[PART : PART + 1] + block[PART + 1 : PART + 2] + block[PART + 2 : PART + 3]
        entering = jnp.exp(log_decay) * entering + block[0:PART]


def scan_part(got):
    return pl.pallas_call(
        scan_kernel, out_shape=jax.ShapeDtypeStruct((32, PART, NS), BF16), name="mixer_scan"
    )(got)


def inner_kernel(skip, xc, bc, cols, rows, out):
    g = dot_tt(bc[:, NS : 2 * NS], bc[:, 0:NS])
    t = lax.broadcasted_iota(jnp.int32, (TOK, TOK), 0)
    s = lax.broadcasted_iota(jnp.int32, (TOK, TOK), 1)
    g = jnp.where(t >= s, g, 0.0)
    lane = lax.broadcasted_iota(jnp.int32, (TOK, 128), 1)
    for j in range(8):
        x = xc[:, 128 * j : 128 * j + 128]
        parts = []
        for h in (2 * j, 2 * j + 1):
            gap = cols[:, HEADS + h : HEADS + h + 1] - rows[h : h + 1, :]
            mix = g * jnp.exp(jnp.minimum(gap, 0.0)) * rows[HEADS + h : HEADS + h + 1, :]
            parts.append(jnp.dot(mix.astype(BF16), x, preferred_element_type=F32))
        gain = lane_pair(lane, skip[2 * j], skip[2 * j + 1])
        out[:, 128 * j : 128 * j + 128] = lane_pair(lane, parts[0], parts[1]) + gain * x.astype(F32)


def inner_part(skip, xc, bc, cols, rows):
    vm = pl.BlockSpec(memory_space=pltpu.VMEM)
    return pl.pallas_call(
        inner_kernel,
        out_shape=jax.ShapeDtypeStruct((TOK, CH), F32),
        in_specs=[pl.BlockSpec(memory_space=pltpu.SMEM), vm, vm, vm, vm],
        name="mixer_inner",
    )(skip, xc, bc, cols, rows)


def project_kernel(place, y0, bc, entering, cols, gates, gain, weight, keep, send, u_ref, normed):
    @pl.when(pl.program_id(0) == 0)
    def _():
        lane = lax.broadcasted_iota(jnp.int32, (TOK, 128), 1)
        c = bc[:, NS : 2 * NS]
        square = jnp.zeros((TOK, 128), F32)
        for j in range(8):
            lo = 128 * j
            carried = dot_tt(c, entering[lo : lo + 128, :])
            h = 2 * HEADS + 2 * j
            decay = lane_pair(lane, cols[:, h : h + 1], cols[:, h + 1 : h + 2])
            y = y0[:, lo : lo + 128] + decay * carried
            z = gates[:, lo : lo + 128].astype(F32)
            u = y * (z * sigmoid(z))
            u_ref[:, lo : lo + 128] = u
            square = square + u * u
        mean = jnp.sum(square, axis=1, keepdims=True) * (1.0 / CH)
        scale = lax.rsqrt(mean + 1e-05)
        core = place[0]
        for d in range(NX * NC):
            first = 32 * (d // NC) + 128 * jnp.where(core == d % NC, 0, 1)
            first = pl.multiple_of(first, 32)
            value = u_ref[32 * d : 32 * d + 32, :] * scale[32 * d : 32 * d + 32] * gain[...]
            normed[pl.ds(first, 32), :] = value.astype(BF16)

    product = jnp.dot(normed[...], weight[...], preferred_element_type=F32).astype(BF16)
    keep[...] = product[0:128]
    send[...] = product[128:256]


def project_part(place, y0, bc, entering, cols, gates, gain, weight):
    block = 512
    whole = lambda *shape: pl.BlockSpec(shape, lambda i, p: (0,) * len(shape))
    half = jax.ShapeDtypeStruct((128, DOUT), BF16)
    return pl.pallas_call(
        project_kernel,
        out_shape=(half, half),
        grid_spec=pltpu.PrefetchScalarGridSpec(
            num_scalar_prefetch=1,
            grid=(DOUT // block,),
            in_specs=[
                whole(TOK, CH),
                whole(TOK, 256),
                whole(CH, NS),
                whole(TOK, 128),
                whole(TOK, CH),
                whole(1, CH),
                pl.BlockSpec((CH, block), lambda i, p: (0, i)),
            ],
            out_specs=[pl.BlockSpec((128, block), lambda i, p: (0, i))] * 2,
            scratch_shapes=[pltpu.VMEM((TOK, CH), F32), pltpu.VMEM((TOK, CH), BF16)],
        ),
        name="mixer_project",
    )(place, y0, bc, entering, cols, gates, gain, weight)


def pair_sum_kernel(place, keep, got, *outs):
    x = place[1]
    for s in range(NX):
        first = pl.multiple_of(((x + s) % NX) * 32, 32)
        total = keep[pl.ds(first, 32), :].astype(F32) + got[pl.ds(first, 32), :].astype(F32)
        outs[s][...] = total.astype(BF16)


def pair_sum(place, keep, got):
    vm = pl.BlockSpec(memory_space=pltpu.VMEM)
    return pl.pallas_call(
        pair_sum_kernel,
        out_shape=(jax.ShapeDtypeStruct((32, DOUT), BF16),) * NX,
        in_specs=[pl.BlockSpec(memory_space=pltpu.SMEM), vm, vm],
        name="pair_sum",
    )(place, keep, got)


def accumulate(q, k, v, state, allowed=None):
    peak, acc = state
    ones = jnp.ones(v.shape, BF16)
    scores = dot_tt(q, k) * (HD**-0.5 * LOG2E)
    if allowed is not None:
        scores = jnp.where(allowed, scores, -1e30)
    new_peak = jnp.maximum(peak, jnp.max(scores, axis=1, keepdims=True))
    weights = jnp.exp2(scores - new_peak).astype(BF16)
    acc = acc * jnp.exp2(peak - new_peak) + jnp.dot(
        weights, jnp.concatenate([v, ones], axis=1), preferred_element_type=F32
    )
    return new_peak, acc


def own_row_kernel(place, q, *refs):
    pieces, (peak_out, acc_out) = refs[:NZ], refs[NZ:]
    z = place[2]
    t = lax.broadcasted_iota(jnp.int32, (TOK, TOK), 0)
    s = lax.broadcasted_iota(jnp.int32, (TOK, TOK), 1)
    qv = q[...]
    own = pieces[0]
    state = (jnp.full((TOK, 1), -1e30, F32), jnp.zeros((TOK, 2 * HD), F32))
    peak, acc = accumulate(qv, own[0:TOK, :], own[TOK : 2 * TOK, :], state, t >= s)
    peak_out[0] = jnp.broadcast_to(peak, (TOK, HD))
    acc_out[0] = acc
    for o in range(1, NZ):

        @pl.when(o <= z)
        def _(piece=pieces[o]):
            peak, acc = accumulate(
                qv, piece[0:TOK, :], piece[TOK : 2 * TOK, :], (peak_out[0, :, 0:1], acc_out[0])
            )
            peak_out[0] = jnp.broadcast_to(peak, (TOK, HD))
            acc_out[0] = acc


STATE = (
    jax.ShapeDtypeStruct((QH, TOK, HD), F32),
    jax.ShapeDtypeStruct((QH, TOK, 2 * HD), F32),
)
STATE_SPECS = [
    pl.BlockSpec((1, TOK, HD), lambda h, p: (h, 0, 0)),
    pl.BlockSpec((1, TOK, 2 * HD), lambda h, p: (h, 0, 0)),
]


def whole_spec(a):
    return pl.BlockSpec(a.shape, lambda h, p: (0,) * a.ndim)


def own_row(place, q, pieces):
    return pl.pallas_call(
        own_row_kernel,
        out_shape=STATE,
        grid_spec=pltpu.PrefetchScalarGridSpec(
            num_scalar_prefetch=1,
            grid=(QH,),
            in_specs=[pl.BlockSpec((TOK, HD), lambda h, p: (0, h))] + [whole_spec(a) for a in pieces],
            out_specs=STATE_SPECS,
        ),
        name="attend_row",
    )(place, q, *pieces)


def rows_kernel(least, final, place, q, *refs):
    n = len(least)
    sets, (peak_in, acc_in), outs = refs[:n], refs[n : n + 2], refs[n + 2 :]
    y = place[3]
    scratch = outs[1:] if final else outs
    peak_out, acc_out = scratch
    peak_out[0] = peak_in[0]
    acc_out[0] = acc_in[0]
    qv = q[...]
    for low, ref in zip(least, sets):

        @pl.when(y >= low)
        def _(ref=ref):
            peak, acc = peak_out[0, :, 0:1], acc_out[0]
            for o in range(0, ref.shape[0], 2):
                k = jnp.concatenate([ref[o, 0:TOK, :], ref[o + 1, 0:TOK, :]], axis=0)
                v = jnp.concatenate([ref[o, TOK : 2 * TOK, :], ref[o + 1, TOK : 2 * TOK, :]], axis=0)
                peak, acc = accumulate(qv, k, v, (peak, acc))
            peak_out[0] = jnp.broadcast_to(peak, (TOK, HD))
            acc_out[0] = acc

    if final:
        acc = acc_out[0]
        outs[0][...] = (acc[:, 0:HD] / acc[:, HD : 2 * HD]).astype(BF16)


def other_rows(place, q, sets, least, state, final):
    specs = [pl.BlockSpec((TOK, HD), lambda h, p: (0, h))] + [whole_spec(a) for a in sets] + STATE_SPECS
    if final:
        out_shape = jax.ShapeDtypeStruct((TOK, QH * HD), BF16)
        out_specs = pl.BlockSpec((TOK, HD), lambda h, p: (0, h))
        scratch = [pltpu.VMEM((1, TOK, HD), F32), pltpu.VMEM((1, TOK, 2 * HD), F32)]
    else:
        out_shape, out_specs, scratch = STATE, STATE_SPECS, []
    return pl.pallas_call(
        functools.partial(rows_kernel, least, final),
        out_shape=out_shape,
        grid_spec=pltpu.PrefetchScalarGridSpec(
            num_scalar_prefetch=1,
            grid=(QH,),
            in_specs=specs,
            out_specs=out_specs,
            scratch_shapes=scratch,
        ),
        name="attend_rows",
    )(place, q, *sets, *state)


def along_z(step):
    return [(y * NZ + z, y * NZ + (z + step) % NZ) for y in range(NY) for z in range(NZ)]


def along_y(pairs):
    return [(a * NZ + z, b * NZ + z) for a, b in pairs for z in range(NZ)]


def along_x(step):
    return [(x * NC + c, ((x + step) % NX) * NC + c) for x in range(NX) for c in range(NC)]


def per_device(
    ssm_inputs,
    state_maps,
    ssm_gates,
    time_steps,
    log_rates,
    skip_gain,
    conv_inputs,
    conv_maps,
    norm_gain,
    out_weight,
    queries,
    attention_keys,
    values,
):
    ctx = lax.axis_index("ctx")
    tp = lax.axis_index("tp")
    place = jnp.stack([tp % NC, tp // NC, ctx % NZ, ctx // NZ]).astype(jnp.int32)
    maps = state_maps.reshape(TOK, 256)
    taps_m = conv_maps.reshape(4, 256)

    edge = jnp.concatenate([ssm_inputs[TOK - 8 :], maps[TOK - 8 :]], axis=1)
    halo = lax.ppermute(edge, "ctx", [(i, i + 1) for i in range(NY * NZ - 1)])
    kv = jnp.concatenate([attention_keys, values], axis=0)
    f1 = lax.ppermute(kv, "ctx", along_z(1))
    b1 = lax.ppermute(kv, "ctx", along_z(-1))
    pack, xc, bc, cols, rows = local_part(
        halo, ssm_inputs, maps, conv_inputs, taps_m, time_steps, log_rates.reshape(1, HEADS)
    )
    f2 = lax.ppermute(f1, "ctx", along_z(1))
    b2 = lax.ppermute(b1, "ctx", along_z(-1))
    got = lax.all_to_all(pack, "ctx", 0, 0)
    f3 = lax.ppermute(f2, "ctx", along_z(1))
    b3 = lax.ppermute(b2, "ctx", along_z(-1))
    f4 = lax.ppermute(f3, "ctx", along_z(1))
    y0 = inner_part(skip_gain, xc, bc, cols, rows)
    entering = lax.all_to_all(scan_part(got), "ctx", 0, 0).reshape(CH, NS)

    pieces = [kv, f1, f2, f3, f4, b3, b2, b1]
    row = jnp.stack(pieces)
    yf = lax.ppermute(row, "ctx", along_y([(0, 1), (1, 2), (2, 3)]))
    yb = lax.ppermute(row, "ctx", along_y([(0, 3), (1, 0)]))
    y2f = lax.ppermute(yf[: NZ // 2], "ctx", along_y([(1, 2), (2, 3)]))
    y2b = lax.ppermute(yb[NZ // 2 :], "ctx", along_y([(3, 2), (0, 3)]))
    state = own_row(place, queries, pieces)
    state = other_rows(place, queries, [yf, yb], [1, 3], state, False)

    keep, send = project_part(
        place, y0, bc, entering, cols, ssm_gates, norm_gain.reshape(1, CH), out_weight
    )
    swapped = lax.ppermute(send, "tp", [(i, i ^ 1) for i in range(NX * NC)])
    sums = pair_sum(place, keep, swapped)
    others = [lax.ppermute(sums[s], "tp", along_x(s)) for s in range(1, NX)]
    total = sums[0].astype(F32)
    for a in others:
        total = total + a.astype(F32)
    ssm_out = total.astype(BF16)

    attn_out = other_rows(place, queries, [y2f, y2b], [2, 2], state, True)
    return ssm_out, attn_out


def solution(mesh):
    placed = (
        P("ctx", "tp"),
        P("ctx", "tp", None),
        P("ctx", "tp"),
        P("tp", "ctx"),
        P("tp"),
        P("tp"),
        P(None, "tp"),
        P(None, "tp", None),
        P("tp"),
        P("tp", None),
        P("ctx", "tp"),
        P("ctx", "tp"),
        P("ctx", "tp"),
    )
    return jax.shard_map(
        per_device,
        mesh=mesh,
        in_specs=placed,
        out_specs=(P(("ctx", "tp"), None), P("ctx", "tp")),
        check_vma=False,
    )
```

```python
import functools

import jax
import jax.numpy as jnp
from jax import lax
from jax.experimental import pallas as pl
from jax.experimental.pallas import tpu as pltpu
from jax.sharding import PartitionSpec as P


F32 = jnp.float32
BF16 = jnp.bfloat16

TOK = 256
CH = 1024
HEADS = 16
NS = 128
NY, NZ = 4, 8
NX, NC = 4, 2
PART = 32
PACK = 48
QH = 8
HD = 128
DOUT = 4096
LOG2E = 1.4426950408889634
PARAMS = pltpu.CompilerParams(vmem_limit_bytes=24 * 2**20)


def dot_tt(a, b):
    return lax.dot_general(a, b, (((1,), (1,)), ((), ())), preferred_element_type=F32)


def lane_pair(lane, left, right):
    return jnp.where(lane < 64, left, right)


def sigmoid(x):
    return 1.0 / (1.0 + jnp.exp(-x))


def local_kernel(halo, xs, maps, taps_x, taps_m, steps, rates, pack, xc, bc, cols, rows, ext):
    ext[0:8, :] = halo[...].astype(F32)
    ext[8 : 8 + TOK, 0:CH] = xs[...].astype(F32)
    ext[8 : 8 + TOK, CH : CH + 256] = maps[...].astype(F32)
    weights_x = taps_x[...].astype(F32)
    weights_m = taps_m[...].astype(F32)

    def conv(lo, width, w):
        total = w[0:1] * ext[5 : 5 + TOK, lo : lo + width]
        for k in range(1, 4):
            total = total + w[k : k + 1] * ext[5 + k : 5 + k + TOK, lo : lo + width]
        return (total * sigmoid(total)).astype(BF16)

    bc[...] = conv(CH, 256, weights_m)
    dt = jax.nn.softplus(steps[...])
    eye = lax.broadcasted_iota(jnp.int32, (HEADS, HEADS), 0) == lax.broadcasted_iota(
        jnp.int32, (HEADS, HEADS), 1
    )
    rate_row = -jnp.exp(rates[...])
    rate = jnp.sum(
        jnp.where(eye, jnp.broadcast_to(rate_row, (HEADS, HEADS)), 0.0), axis=1, keepdims=True
    )
    cum = dt * rate
    token = lax.broadcasted_iota(jnp.int32, (HEADS, TOK), 1)
    for s in (1, 2, 4, 8, 16, 32, 64, 128):
        cum = cum + jnp.where(token >= s, pltpu.roll(cum, s, 1), 0.0)
    total = cum[:, TOK - 1 : TOK]
    tail = jnp.exp(total - cum) * dt
    rows[0:HEADS, :] = cum
    rows[HEADS : 2 * HEADS, :] = dt
    stacked = jnp.concatenate(
        [tail, cum, jnp.exp(cum), jnp.zeros((128 - 3 * HEADS, TOK), F32)], axis=0
    )
    columns = jnp.transpose(stacked)
    cols[...] = columns
    lane = lax.broadcasted_iota(jnp.int32, (TOK, 128), 1)
    b = bc[:, 0:NS]
    for j in range(8):
        lo = 128 * j
        x = conv(lo, 128, weights_x[:, lo : lo + 128])
        xc[:, lo : lo + 128] = x
        tail_pair = lane_pair(lane, columns[:, 2 * j : 2 * j + 1], columns[:, 2 * j + 1 : 2 * j + 2])
        weighted = (tail_pair * x.astype(F32)).astype(BF16)
        state = lax.dot_general(
            weighted, b, (((0,), (0,)), ((), ())), preferred_element_type=F32
        )
        pack[4 * j : 4 * j + 4, 0:PART, :] = state.astype(BF16).reshape(4, PART, NS)
    row = lax.broadcasted_iota(jnp.int32, (PACK - PART, NS), 0)
    hi = total.astype(BF16).astype(F32)
    mid = (total - hi).astype(BF16).astype(F32)
    low = total - hi - mid
    for h in range(HEADS):
        piece = jnp.where(
            row == 0,
            hi[h : h + 1, :],
            jnp.where(row == 1, mid[h : h + 1, :], jnp.where(row == 2, low[h : h + 1, :], 0.0)),
        ).astype(BF16)
        pack[2 * h, PART:PACK, :] = piece
        pack[2 * h + 1, PART:PACK, :] = piece


def local_part(halo, xs, maps, taps_x, taps_m, steps, rates):
    return pl.pallas_call(
        local_kernel,
        out_shape=(
            jax.ShapeDtypeStruct((32, PACK, NS), BF16),
            jax.ShapeDtypeStruct((TOK, CH), BF16),
            jax.ShapeDtypeStruct((TOK, 256), BF16),
            jax.ShapeDtypeStruct((TOK, 128), F32),
            jax.ShapeDtypeStruct((2 * HEADS, TOK), F32),
        ),
        scratch_shapes=[pltpu.VMEM((TOK + 8, CH + 256), F32)],
        compiler_params=PARAMS,
        name="mixer_local",
    )(*[in_hbm(a) for a in (halo, xs, maps, taps_x, taps_m, steps, rates)])


def scan_kernel(got, out):
    entering = jnp.zeros((PART, NS), F32)
    for b in range(NY * NZ):
        out[b] = entering.astype(BF16)
        block = got[b].astype(F32)
        log_decay = block[PART : PART + 1] + block[PART + 1 : PART + 2] + block[PART + 2 : PART + 3]
        entering = jnp.exp(log_decay) * entering + block[0:PART]


def scan_part(got):
    return pl.pallas_call(
        scan_kernel, out_shape=jax.ShapeDtypeStruct((32, PART, NS), BF16), compiler_params=PARAMS, name="mixer_scan"
    )(got)


def inner_kernel(skip, xc, bc, cols, rows, out):
    g = dot_tt(bc[:, NS : 2 * NS], bc[:, 0:NS])
    t = lax.broadcasted_iota(jnp.int32, (TOK, TOK), 0)
    s = lax.broadcasted_iota(jnp.int32, (TOK, TOK), 1)
    g = jnp.where(t >= s, g, 0.0)
    lane = lax.broadcasted_iota(jnp.int32, (TOK, 128), 1)
    for j in range(8):
        x = xc[:, 128 * j : 128 * j + 128]
        parts = []
        for h in (2 * j, 2 * j + 1):
            gap = cols[:, HEADS + h : HEADS + h + 1] - rows[h : h + 1, :]
            mix = g * jnp.exp(jnp.minimum(gap, 0.0)) * rows[HEADS + h : HEADS + h + 1, :]
            parts.append(jnp.dot(mix.astype(BF16), x, preferred_element_type=F32))
        gain = lane_pair(lane, skip[2 * j], skip[2 * j + 1])
        out[:, 128 * j : 128 * j + 128] = lane_pair(lane, parts[0], parts[1]) + gain * x.astype(F32)


def inner_part(skip, xc, bc, cols, rows):
    vm = pl.BlockSpec(memory_space=pltpu.VMEM)
    return pl.pallas_call(
        inner_kernel,
        out_shape=jax.ShapeDtypeStruct((TOK, CH), F32),
        in_specs=[pl.BlockSpec(memory_space=pltpu.SMEM), vm, vm, vm, vm],
        compiler_params=PARAMS,
        name="mixer_inner",
    )(skip, xc, bc, cols, rows)


def project_kernel(place, y0, bc, entering, cols, gates, gain, weight, keep, send, u_ref, normed, wbuf, sems):
    block = wbuf.shape[2]
    copies = [
        pltpu.make_async_copy(weight.at[:, pl.ds(block * i, block)], wbuf.at[i], sems.at[i])
        for i in range(wbuf.shape[0])
    ]
    for copy in copies:
        copy.start()
    lane = lax.broadcasted_iota(jnp.int32, (TOK, 128), 1)
    c = bc[:, NS : 2 * NS]
    square = jnp.zeros((TOK, 128), F32)
    for j in range(8):
        lo = 128 * j
        carried = dot_tt(c, entering[lo : lo + 128, :])
        h = 2 * HEADS + 2 * j
        decay = lane_pair(lane, cols[:, h : h + 1], cols[:, h + 1 : h + 2])
        y = y0[:, lo : lo + 128] + decay * carried
        z = gates[:, lo : lo + 128].astype(F32)
        u = y * (z * sigmoid(z))
        u_ref[:, lo : lo + 128] = u
        square = square + u * u
    mean = jnp.sum(square, axis=1, keepdims=True) * (1.0 / CH)
    scale = lax.rsqrt(mean + 1e-05)
    core = place[0]
    for d in range(NX * NC):
        first = 32 * (d // NC) + 128 * jnp.where(core == d % NC, 0, 1)
        first = pl.multiple_of(first, 32)
        value = u_ref[32 * d : 32 * d + 32, :] * scale[32 * d : 32 * d + 32] * gain[...]
        normed[pl.ds(first, 32), :] = value.astype(BF16)
    rows = normed[...]
    for i, copy in enumerate(copies):
        copy.wait()
        product = jnp.dot(rows, wbuf[i], preferred_element_type=F32).astype(BF16)
        keep[:, block * i : block * i + block] = product[0:128]
        send[:, block * i : block * i + block] = product[128:256]


def project_part(place, y0, bc, entering, cols, gates, gain, weight):
    block = 1024
    vm = pl.BlockSpec(memory_space=pltpu.VMEM)
    half = jax.ShapeDtypeStruct((128, DOUT), BF16)
    return pl.pallas_call(
        project_kernel,
        out_shape=(half, half),
        in_specs=[pl.BlockSpec(memory_space=pltpu.SMEM)] + [vm] * 6 + [pl.BlockSpec(memory_space=pl.ANY)],
        scratch_shapes=[
            pltpu.VMEM((TOK, CH), F32),
            pltpu.VMEM((TOK, CH), BF16),
            pltpu.VMEM((DOUT // block, CH, block), BF16),
            pltpu.SemaphoreType.DMA((DOUT // block,)),
        ],
        compiler_params=PARAMS,
        name="mixer_project",
    )(place, y0, bc, entering, cols, gates, gain, in_hbm(weight))


def pair_sum_kernel(place, keep, got, *outs):
    x = place[1]
    for s in range(NX):
        first = pl.multiple_of(((x + s) % NX) * 32, 32)
        total = keep[pl.ds(first, 32), :].astype(F32) + got[pl.ds(first, 32), :].astype(F32)
        outs[s][...] = total.astype(BF16)


def pair_sum(place, keep, got):
    vm = pl.BlockSpec(memory_space=pltpu.VMEM)
    return pl.pallas_call(
        pair_sum_kernel,
        out_shape=(jax.ShapeDtypeStruct((32, DOUT), BF16),) * NX,
        in_specs=[pl.BlockSpec(memory_space=pltpu.SMEM), vm, vm],
        compiler_params=PARAMS,
        name="pair_sum",
    )(place, keep, got)


def prep_kernel(xs, maps, k, v, edge, kv):
    edge[:, 0:CH] = xs[...]
    edge[:, CH : CH + 256] = maps[...]
    kv[0:TOK, :] = k[...]
    for i in range(2):
        turned = jnp.transpose(v[128 * i : 128 * i + 128, :].astype(F32))
        kv[TOK + 128 * i : TOK + 128 * i + 128, :] = turned.astype(BF16)


def prep(xs, maps, k, v):
    last = lambda width: pl.BlockSpec((8, width), lambda i: (TOK // 8 - 1, 0))
    full = lambda rows, width: pl.BlockSpec((rows, width), lambda i: (0, 0))
    return pl.pallas_call(
        prep_kernel,
        grid=(1,),
        out_shape=(
            jax.ShapeDtypeStruct((8, CH + 256), BF16),
            jax.ShapeDtypeStruct((2 * TOK, HD), BF16),
        ),
        in_specs=[last(CH), last(256), full(TOK, HD), full(TOK, HD)],
        out_specs=[full(8, CH + 256), full(2 * TOK, HD)],
        compiler_params=PARAMS,
        name="prep",
    )(in_hbm(xs), in_hbm(maps), in_hbm(k), in_hbm(v))


def stack_kernel(*refs):
    for i in range(NZ):
        refs[NZ + i // 4][i % 4] = refs[i][...]


def stack(pieces):
    part = pl.BlockSpec((256, HD), lambda i: (i, 0))
    return pl.pallas_call(
        stack_kernel,
        grid=(2,),
        out_shape=(jax.ShapeDtypeStruct((NZ // 2, 2 * TOK, HD), BF16),) * 2,
        in_specs=[part] * NZ,
        out_specs=[pl.BlockSpec((NZ // 2, 256, HD), lambda i: (0, i, 0))] * 2,
        compiler_params=PARAMS,
        name="stack_row",
    )(*[in_hbm(a) for a in pieces])


GH = 4
AHEAD = 3
ACC = HD + 8
VM = pl.BlockSpec(memory_space=pltpu.VMEM)
SM = pl.BlockSpec(memory_space=pltpu.SMEM)


def in_hbm(x):
    return pltpu.with_memory_space_constraint(x, pltpu.HBM)


def in_vmem(x):
    return pltpu.with_memory_space_constraint(x, pltpu.VMEM)


def attend(queries, chunks, peaks, accs):
    heads = [(q.astype(F32) * (HD**-0.5 * LOG2E)).astype(BF16) for q in queries]
    steps = [(chunk, g) for chunk in chunks for g in range(GH)]

    def scores(step):
        (pieces, mask), g = step
        k = [p[0:TOK, :] for p in pieces]
        s = dot_tt(k[0] if len(k) == 1 else jnp.concatenate(k, axis=0), heads[g])
        return s if mask is None else mask(s)

    waiting = [scores(step) for step in steps[:AHEAD]]
    for i, ((pieces, _), g) in enumerate(steps):
        if i + AHEAD < len(steps):
            waiting.append(scores(steps[i + AHEAD]))
        s = waiting.pop(0)
        n = s.shape[0]
        best = jnp.max(s.reshape(n // 8, 8, TOK), axis=0)
        best = jnp.broadcast_to(jnp.max(best, axis=0, keepdims=True), (8, TOK))
        peak = jnp.maximum(peaks[g], best)
        weights = jnp.exp2(s - peak[0:1]).astype(BF16)
        old = accs[g] * jnp.exp2(peaks[g] - peak)[0:1]
        peaks[g] = peak
        turned = []
        for p in pieces:
            turned += [p[TOK : TOK + 128, :], p[TOK + 128 : TOK + 256, :]]
        turned = jnp.concatenate([jnp.concatenate(turned, axis=1), jnp.ones((8, n), BF16)], axis=0)
        accs[g] = old + jnp.dot(turned, weights, preferred_element_type=F32)


def head_lanes(group, g):
    return pl.ds(pl.multiple_of(GH * HD * group + HD * g, HD), HD)


def attend_group(group, q, chunks, state):
    peak, acc = state
    queries = [q[:, head_lanes(group, g)] for g in range(GH)]
    peaks = [peak[GH * group + g] for g in range(GH)]
    accs = [acc[GH * group + g] for g in range(GH)]
    attend(queries, chunks, peaks, accs)
    for g in range(GH):
        peak[GH * group + g] = peaks[g]
        acc[GH * group + g] = accs[g]


STATE = (pltpu.VMEM((QH, 8, TOK), F32), pltpu.VMEM((QH, ACC, TOK), F32))


def own_row_kernel(place, q, *refs):
    pieces, state = refs[:NZ], refs[NZ:]
    z = place[2]

    def diagonal(s):
        key = lax.broadcasted_iota(jnp.int32, (TOK, TOK), 0)
        query = lax.broadcasted_iota(jnp.int32, (TOK, TOK), 1)
        return jnp.where(key <= query, s, -1e30)

    def before(offs):
        def mask(s):
            parts = [jnp.where(o <= z, s[TOK * i : TOK * i + TOK], -1e30) for i, o in enumerate(offs)]
            return parts[0] if len(parts) == 1 else jnp.concatenate(parts, axis=0)

        return mask

    state[0][...] = jnp.full((QH, 8, TOK), -1e30, F32)
    state[1][...] = jnp.zeros((QH, ACC, TOK), F32)
    chunks = [([pieces[0]], diagonal)]
    for o in range(1, NZ, 2):
        offs = range(o, min(o + 2, NZ))
        chunks.append(([pieces[i] for i in offs], before(offs)))

    @pl.loop(0, QH // GH)
    def _(group):
        attend_group(group, q, chunks, state)


def own_row(place, q, pieces):
    return pl.pallas_call(
        own_row_kernel,
        out_shape=STATE,
        in_specs=[SM] + [VM] * (1 + NZ),
        out_specs=[VM, VM],
        compiler_params=PARAMS,
        name="attend_row",
    )(place, q, *[in_hbm(a) for a in pieces])


def rows_kernel(least, final, place, q, *refs):
    n = len(least)
    sets, outs = refs[:n], refs[n + 2 :]
    state = outs[-2:]
    y = place[3]

    for low in sorted(set(least)):

        @pl.when(y >= low)
        def _(low=low):
            pieces = [ref.at[o] for ref, at in zip(sets, least) if at == low for o in range(ref.shape[0])]
            chunks = [(pieces[o : o + 2], None) for o in range(0, len(pieces), 2)]

            @pl.loop(0, QH // GH)
            def _(group):
                attend_group(group, q, chunks, state)

    if final:
        for h in range(QH):
            value = state[1][h, 0:HD, :] / state[1][h, HD : HD + 1, :]
            outs[0][:, HD * h : HD * h + HD] = jnp.transpose(value).astype(BF16)


def other_rows(place, q, sets, least, state, final=False):
    first = 2 + len(sets)
    head = (jax.ShapeDtypeStruct((TOK, QH * HD), BF16),) if final else ()
    return pl.pallas_call(
        functools.partial(rows_kernel, least, final),
        out_shape=head + STATE,
        in_specs=[SM] + [VM] * (3 + len(sets)),
        out_specs=[VM] * (len(head) + 2),
        input_output_aliases={first: len(head), first + 1: len(head) + 1},
        compiler_params=PARAMS,
        name="attend_final" if final else "attend_rows",
    )(place, q, *[in_hbm(a) for a in sets], *[in_vmem(a) for a in state])


def along_z(step):
    return [(y * NZ + z, y * NZ + (z + step) % NZ) for y in range(NY) for z in range(NZ)]


def along_y(pairs):
    return [(a * NZ + z, b * NZ + z) for a, b in pairs for z in range(NZ)]


def along_x(step):
    return [(x * NC + c, ((x + step) % NX) * NC + c) for x in range(NX) for c in range(NC)]


def per_device(
    ssm_inputs,
    state_maps,
    ssm_gates,
    time_steps,
    log_rates,
    skip_gain,
    conv_inputs,
    conv_maps,
    norm_gain,
    out_weight,
    queries,
    attention_keys,
    values,
):
    ctx = lax.axis_index("ctx")
    tp = lax.axis_index("tp")
    place = jnp.stack([tp % NC, tp // NC, ctx % NZ, ctx // NZ]).astype(jnp.int32)
    maps = state_maps.reshape(TOK, 256)
    taps_m = conv_maps.reshape(4, 256)

    edge, kv = prep(ssm_inputs, maps, attention_keys, values)
    halo = lax.ppermute(edge, "ctx", [(i, i + 1) for i in range(NY * NZ - 1)])
    f1 = lax.ppermute(kv, "ctx", along_z(1))
    b1 = lax.ppermute(kv, "ctx", along_z(-1))
    pack, xc, bc, cols, rows = local_part(
        halo, ssm_inputs, maps, conv_inputs, taps_m, time_steps, log_rates.reshape(1, HEADS)
    )
    f2 = lax.ppermute(f1, "ctx", along_z(1))
    b2 = lax.ppermute(b1, "ctx", along_z(-1))
    got = lax.all_to_all(pack, "ctx", 0, 0)
    f3 = lax.ppermute(f2, "ctx", along_z(1))
    b3 = lax.ppermute(b2, "ctx", along_z(-1))
    y0 = inner_part(skip_gain, xc, bc, cols, rows)
    f4 = lax.ppermute(f3, "ctx", along_z(1))
    scanned = scan_part(got)
    entering = lax.all_to_all(scanned, "ctx", 0, 0).reshape(CH, NS)

    pieces = [kv, f1, f2, f3, f4, b3, b2, b1]
    near, far = stack(pieces)
    up, down = along_y([(0, 1), (1, 2), (2, 3)]), along_y([(0, 3), (1, 0)])
    yfa = lax.ppermute(near, "ctx", up)
    yba = lax.ppermute(far, "ctx", down)
    state = own_row(place, queries, pieces)
    y2f = lax.ppermute(yfa, "ctx", along_y([(1, 2), (2, 3)]))
    y2b = lax.ppermute(yba, "ctx", along_y([(3, 2), (0, 3)]))
    yfb = lax.ppermute(far, "ctx", up)
    ybb = lax.ppermute(near, "ctx", along_y([(0, 3)]))
    state = other_rows(place, queries, [yfa, yba], [1, 3], state)
    keep, send = project_part(
        place, y0, bc, entering, cols, ssm_gates, norm_gain.reshape(1, CH), out_weight
    )
    swapped = lax.ppermute(send, "tp", [(i, i ^ 1) for i in range(NX * NC)])
    state = other_rows(place, queries, [yfb, ybb], [1, 3], state)
    sums = pair_sum(place, keep, swapped)
    others = []
    for s in range(1, NX):
        others.append(lax.ppermute(sums[s], "tp", along_x(s)))
    attn_out, *_ = other_rows(place, queries, [y2f, y2b], [2, 2], state, final=True)
    total = sums[0].astype(F32)
    for a in others:
        total = total + a.astype(F32)
    ssm_out = total.astype(BF16)
    return ssm_out, attn_out


def solution(mesh):
    placed = (
        P("ctx", "tp"),
        P("ctx", "tp", None),
        P("ctx", "tp"),
        P("tp", "ctx"),
        P("tp"),
        P("tp"),
        P(None, "tp"),
        P(None, "tp", None),
        P("tp"),
        P("tp", None),
        P("ctx", "tp"),
        P("ctx", "tp"),
        P("ctx", "tp"),
    )

    return jax.shard_map(
        per_device,
        mesh=mesh,
        in_specs=placed,
        out_specs=(P(("ctx", "tp"), None), P("ctx", "tp")),
        check_vma=False,
    )
```

```python
import functools

import jax
import jax.numpy as jnp
from jax import lax
from jax.experimental import pallas as pl
from jax.experimental.pallas import tpu as pltpu
from jax.sharding import PartitionSpec as P


F32 = jnp.float32
BF16 = jnp.bfloat16

TOK = 256
CH = 1024
HEADS = 16
NS = 128
NY, NZ = 4, 8
NX, NC = 4, 2
PART = 32
PACK = 40
QH = 8
HD = 128
DOUT = 4096
LOG2E = 1.4426950408889634
PARAMS = pltpu.CompilerParams(vmem_limit_bytes=24 * 2**20)


def dot_tt(a, b):
    return lax.dot_general(a, b, (((1,), (1,)), ((), ())), preferred_element_type=F32)


def lane_pair(lane, left, right):
    return jnp.where(lane < 64, left, right)


def sigmoid(x):
    return 1.0 / (1.0 + jnp.exp(-x))


def local_kernel(halo, xs, maps, taps_x, taps_m, steps, rates, pack, xc, bc, cols, rows, ext):
    ext[0:8, :] = halo[...].astype(F32)
    ext[8 : 8 + TOK, 0:CH] = xs[...].astype(F32)
    ext[8 : 8 + TOK, CH : CH + 256] = maps[...].astype(F32)
    weights_x = taps_x[...].astype(F32)
    weights_m = taps_m[...].astype(F32)

    def conv(lo, width, w):
        total = w[0:1] * ext[5 : 5 + TOK, lo : lo + width]
        for k in range(1, 4):
            total = total + w[k : k + 1] * ext[5 + k : 5 + k + TOK, lo : lo + width]
        return (total * sigmoid(total)).astype(BF16)

    bc[...] = conv(CH, 256, weights_m)
    dt = jax.nn.softplus(steps[...])
    eye = lax.broadcasted_iota(jnp.int32, (HEADS, HEADS), 0) == lax.broadcasted_iota(
        jnp.int32, (HEADS, HEADS), 1
    )
    rate_row = -jnp.exp(rates[...])
    rate = jnp.sum(
        jnp.where(eye, jnp.broadcast_to(rate_row, (HEADS, HEADS)), 0.0), axis=1, keepdims=True
    )
    cum = dt * rate
    token = lax.broadcasted_iota(jnp.int32, (HEADS, TOK), 1)
    for s in (1, 2, 4, 8, 16, 32, 64, 128):
        cum = cum + jnp.where(token >= s, pltpu.roll(cum, s, 1), 0.0)
    total = cum[:, TOK - 1 : TOK]
    tail = jnp.exp(total - cum) * dt
    rows[0:HEADS, :] = cum
    rows[HEADS : 2 * HEADS, :] = dt
    stacked = jnp.concatenate(
        [tail, cum, jnp.exp(cum), jnp.zeros((128 - 3 * HEADS, TOK), F32)], axis=0
    )
    columns = jnp.transpose(stacked)
    cols[...] = columns
    lane = lax.broadcasted_iota(jnp.int32, (TOK, 128), 1)
    b = bc[:, 0:NS]
    for j in range(8):
        lo = 128 * j
        x = conv(lo, 128, weights_x[:, lo : lo + 128])
        xc[:, lo : lo + 128] = x
        tail_pair = lane_pair(lane, columns[:, 2 * j : 2 * j + 1], columns[:, 2 * j + 1 : 2 * j + 2])
        weighted = (tail_pair * x.astype(F32)).astype(BF16)
        state = lax.dot_general(
            weighted, b, (((0,), (0,)), ((), ())), preferred_element_type=F32
        )
        pack[4 * j : 4 * j + 4, 0:PART, :] = state.astype(BF16).reshape(4, PART, NS)
    row = lax.broadcasted_iota(jnp.int32, (PACK - PART, NS), 0)
    hi = total.astype(BF16).astype(F32)
    mid = (total - hi).astype(BF16).astype(F32)
    low = total - hi - mid
    for h in range(HEADS):
        piece = jnp.where(
            row == 0,
            hi[h : h + 1, :],
            jnp.where(row == 1, mid[h : h + 1, :], jnp.where(row == 2, low[h : h + 1, :], 0.0)),
        ).astype(BF16)
        pack[2 * h, PART:PACK, :] = piece
        pack[2 * h + 1, PART:PACK, :] = piece


def local_part(halo, xs, maps, taps_x, taps_m, steps, rates):
    return pl.pallas_call(
        local_kernel,
        out_shape=(
            jax.ShapeDtypeStruct((32, PACK, NS), BF16),
            jax.ShapeDtypeStruct((TOK, CH), BF16),
            jax.ShapeDtypeStruct((TOK, 256), BF16),
            jax.ShapeDtypeStruct((TOK, 128), F32),
            jax.ShapeDtypeStruct((2 * HEADS, TOK), F32),
        ),
        scratch_shapes=[pltpu.VMEM((TOK + 8, CH + 256), F32)],
        compiler_params=PARAMS,
        name="mixer_local",
    )(*[in_hbm(a) for a in (halo, xs, maps, taps_x, taps_m, steps, rates)])


def scan_kernel(got, out):
    entering = jnp.zeros((PART, NS), F32)
    for b in range(NY * NZ):
        out[b] = entering.astype(BF16)
        block = got[b].astype(F32)
        log_decay = block[PART : PART + 1] + block[PART + 1 : PART + 2] + block[PART + 2 : PART + 3]
        entering = jnp.exp(log_decay) * entering + block[0:PART]


def scan_part(got):
    return pl.pallas_call(
        scan_kernel, out_shape=jax.ShapeDtypeStruct((32, PART, NS), BF16), compiler_params=PARAMS, name="mixer_scan"
    )(got)


def inner_kernel(skip, xc, bc, cols, rows, out):
    g = dot_tt(bc[:, NS : 2 * NS], bc[:, 0:NS])
    t = lax.broadcasted_iota(jnp.int32, (TOK, TOK), 0)
    s = lax.broadcasted_iota(jnp.int32, (TOK, TOK), 1)
    g = jnp.where(t >= s, g, 0.0)
    lane = lax.broadcasted_iota(jnp.int32, (TOK, 128), 1)
    for j in range(8):
        x = xc[:, 128 * j : 128 * j + 128]
        parts = []
        for h in (2 * j, 2 * j + 1):
            gap = cols[:, HEADS + h : HEADS + h + 1] - rows[h : h + 1, :]
            mix = g * jnp.exp(jnp.minimum(gap, 0.0)) * rows[HEADS + h : HEADS + h + 1, :]
            parts.append(jnp.dot(mix.astype(BF16), x, preferred_element_type=F32))
        gain = lane_pair(lane, skip[2 * j], skip[2 * j + 1])
        out[:, 128 * j : 128 * j + 128] = lane_pair(lane, parts[0], parts[1]) + gain * x.astype(F32)


def inner_part(skip, xc, bc, cols, rows):
    vm = pl.BlockSpec(memory_space=pltpu.VMEM)
    return pl.pallas_call(
        inner_kernel,
        out_shape=jax.ShapeDtypeStruct((TOK, CH), F32),
        in_specs=[pl.BlockSpec(memory_space=pltpu.SMEM), vm, vm, vm, vm],
        compiler_params=PARAMS,
        name="mixer_inner",
    )(skip, xc, bc, cols, rows)


def project_kernel(place, y0, bc, entering, cols, gates, gain, weight, keep, send, u_ref, normed, wbuf, sems):
    block = wbuf.shape[2]
    copies = [
        pltpu.make_async_copy(weight.at[:, pl.ds(block * i, block)], wbuf.at[i], sems.at[i])
        for i in range(wbuf.shape[0])
    ]
    for copy in copies:
        copy.start()
    lane = lax.broadcasted_iota(jnp.int32, (TOK, 128), 1)
    c = bc[:, NS : 2 * NS]
    square = jnp.zeros((TOK, 128), F32)
    for j in range(8):
        lo = 128 * j
        carried = dot_tt(c, entering[lo : lo + 128, :])
        h = 2 * HEADS + 2 * j
        decay = lane_pair(lane, cols[:, h : h + 1], cols[:, h + 1 : h + 2])
        y = y0[:, lo : lo + 128] + decay * carried
        z = gates[:, lo : lo + 128].astype(F32)
        u = y * (z * sigmoid(z))
        u_ref[:, lo : lo + 128] = u
        square = square + u * u
    mean = jnp.sum(square, axis=1, keepdims=True) * (1.0 / CH)
    scale = lax.rsqrt(mean + 1e-05)
    core = place[0]
    for d in range(NX * NC):
        first = 32 * (d // NC) + 128 * jnp.where(core == d % NC, 0, 1)
        first = pl.multiple_of(first, 32)
        value = u_ref[32 * d : 32 * d + 32, :] * scale[32 * d : 32 * d + 32] * gain[...]
        normed[pl.ds(first, 32), :] = value.astype(BF16)
    rows = normed[...]
    for i, copy in enumerate(copies):
        copy.wait()
        product = jnp.dot(rows, wbuf[i], preferred_element_type=F32).astype(BF16)
        keep[:, block * i : block * i + block] = product[0:128]
        send[:, block * i : block * i + block] = product[128:256]


def project_part(place, y0, bc, entering, cols, gates, gain, weight):
    block = 1024
    vm = pl.BlockSpec(memory_space=pltpu.VMEM)
    half = jax.ShapeDtypeStruct((128, DOUT), BF16)
    return pl.pallas_call(
        project_kernel,
        out_shape=(half, half),
        in_specs=[pl.BlockSpec(memory_space=pltpu.SMEM)] + [vm] * 6 + [pl.BlockSpec(memory_space=pl.ANY)],
        scratch_shapes=[
            pltpu.VMEM((TOK, CH), F32),
            pltpu.VMEM((TOK, CH), BF16),
            pltpu.VMEM((DOUT // block, CH, block), BF16),
            pltpu.SemaphoreType.DMA((DOUT // block,)),
        ],
        compiler_params=PARAMS,
        name="mixer_project",
    )(place, y0, bc, entering, cols, gates, gain, in_hbm(weight))


def pair_sum_kernel(place, keep, got, *outs):
    x = place[1]
    for s in range(NX):
        first = pl.multiple_of(((x + s) % NX) * 32, 32)
        total = keep[pl.ds(first, 32), :].astype(F32) + got[pl.ds(first, 32), :].astype(F32)
        outs[s][...] = total.astype(BF16)


def pair_sum(place, keep, got):
    vm = pl.BlockSpec(memory_space=pltpu.VMEM)
    return pl.pallas_call(
        pair_sum_kernel,
        out_shape=(jax.ShapeDtypeStruct((32, DOUT), BF16),) * NX,
        in_specs=[pl.BlockSpec(memory_space=pltpu.SMEM), vm, vm],
        compiler_params=PARAMS,
        name="pair_sum",
    )(place, keep, got)


def prep_kernel(xs, maps, k, v, edge, kv):
    edge[:, 0:CH] = xs[...]
    edge[:, CH : CH + 256] = maps[...]
    kv[0:TOK, :] = k[...]
    for i in range(2):
        turned = jnp.transpose(v[128 * i : 128 * i + 128, :].astype(F32))
        kv[TOK + 128 * i : TOK + 128 * i + 128, :] = turned.astype(BF16)


def prep(xs, maps, k, v):
    last = lambda width: pl.BlockSpec((8, width), lambda i: (TOK // 8 - 1, 0))
    full = lambda rows, width: pl.BlockSpec((rows, width), lambda i: (0, 0))
    return pl.pallas_call(
        prep_kernel,
        grid=(1,),
        out_shape=(
            jax.ShapeDtypeStruct((8, CH + 256), BF16),
            jax.ShapeDtypeStruct((2 * TOK, HD), BF16),
        ),
        in_specs=[last(CH), last(256), full(TOK, HD), full(TOK, HD)],
        out_specs=[full(8, CH + 256), full(2 * TOK, HD)],
        compiler_params=PARAMS,
        name="prep",
    )(in_hbm(xs), in_hbm(maps), in_hbm(k), in_hbm(v))


def stack_kernel(*refs):
    for i in range(NZ):
        refs[NZ + i // 4][i % 4] = refs[i][...]


def stack(pieces):
    part = pl.BlockSpec((256, HD), lambda i: (i, 0))
    return pl.pallas_call(
        stack_kernel,
        grid=(2,),
        out_shape=(jax.ShapeDtypeStruct((NZ // 2, 2 * TOK, HD), BF16),) * 2,
        in_specs=[part] * NZ,
        out_specs=[pl.BlockSpec((NZ // 2, 256, HD), lambda i: (0, i, 0))] * 2,
        compiler_params=PARAMS,
        name="stack_row",
    )(*[in_hbm(a) for a in pieces])


AHEAD = 3
ACC = HD + 8
VM = pl.BlockSpec(memory_space=pltpu.VMEM)
SM = pl.BlockSpec(memory_space=pltpu.SMEM)


def in_hbm(x):
    return pltpu.with_memory_space_constraint(x, pltpu.HBM)


def in_vmem(x):
    return pltpu.with_memory_space_constraint(x, pltpu.VMEM)


def attend(queries, chunks, peaks, accs):
    heads = [(q.astype(F32) * (HD**-0.5 * LOG2E)).astype(BF16) for q in queries]
    steps = [(chunk, g) for chunk in chunks for g in range(len(heads))]

    def scores(step):
        (pieces, mask), g = step
        k = [p[0:TOK, :] for p in pieces]
        s = dot_tt(k[0] if len(k) == 1 else jnp.concatenate(k, axis=0), heads[g])
        return s if mask is None else mask(s)

    waiting = [scores(step) for step in steps[:AHEAD]]
    for i, ((pieces, _), g) in enumerate(steps):
        if i + AHEAD < len(steps):
            waiting.append(scores(steps[i + AHEAD]))
        s = waiting.pop(0)
        n = s.shape[0]
        best = jnp.max(s.reshape(n // 8, 8, TOK), axis=0)
        best = jnp.broadcast_to(jnp.max(best, axis=0, keepdims=True), (8, TOK))
        peak = jnp.maximum(peaks[g], best)
        weights = jnp.exp2(s - peak[0:1]).astype(BF16)
        old = accs[g] * jnp.exp2(peaks[g] - peak)[0:1]
        peaks[g] = peak
        turned = []
        for p in pieces:
            turned += [p[TOK : TOK + 128, :], p[TOK + 128 : TOK + 256, :]]
        turned = jnp.concatenate([jnp.concatenate(turned, axis=1), jnp.ones((8, n), BF16)], axis=0)
        accs[g] = old + jnp.dot(turned, weights, preferred_element_type=F32)


def attend_all(together, q, chunks, state):
    peak, acc = state

    @pl.loop(0, QH // together)
    def _(group):
        first = together * group
        lanes = [pl.ds(pl.multiple_of(HD * (first + g), HD), HD) for g in range(together)]
        peaks = [peak[first + g] for g in range(together)]
        accs = [acc[first + g] for g in range(together)]
        attend([q[:, at] for at in lanes], chunks, peaks, accs)
        for g in range(together):
            peak[first + g] = peaks[g]
            acc[first + g] = accs[g]


STATE = (pltpu.VMEM((QH, 8, TOK), F32), pltpu.VMEM((QH, ACC, TOK), F32))


def own_row_kernel(offsets, place, q, *refs):
    n = len(offsets)
    pieces, state = refs[:n], refs[-2:]
    z = place[2]

    def diagonal(s):
        key = lax.broadcasted_iota(jnp.int32, (TOK, TOK), 0)
        query = lax.broadcasted_iota(jnp.int32, (TOK, TOK), 1)
        return jnp.where(key <= query, s, -1e30)

    def before(offs):
        def mask(s):
            parts = [jnp.where(o <= z, s[TOK * i : TOK * i + TOK], -1e30) for i, o in enumerate(offs)]
            return parts[0] if len(parts) == 1 else jnp.concatenate(parts, axis=0)

        return mask

    chunks = []
    at = 0
    if offsets[0] == 0:
        at = 1
        chunks.append(([pieces[0]], diagonal))
        state[0][...] = jnp.full((QH, 8, TOK), -1e30, F32)
        state[1][...] = jnp.zeros((QH, ACC, TOK), F32)
    for o in range(at, n, 2):
        chunks.append((list(pieces[o : o + 2]), before(offsets[o : o + 2])))

    attend_all(QH, q, chunks, state)


def own_row(place, q, pieces, offsets, state=()):
    first = 2 + len(pieces)
    return pl.pallas_call(
        functools.partial(own_row_kernel, offsets),
        out_shape=STATE,
        in_specs=[SM] + [VM] * (1 + len(pieces) + len(state)),
        out_specs=[VM, VM],
        input_output_aliases={first: 0, first + 1: 1} if state else {},
        compiler_params=PARAMS,
        name="attend_row",
    )(place, q, *[in_hbm(a) for a in pieces], *[in_vmem(a) for a in state])


def rows_kernel(least, final, place, q, *refs):
    n = len(least)
    sets, outs = refs[:n], refs[n + 2 :]
    state = outs[-2:]
    y = place[3]

    for low in sorted(set(least)):

        @pl.when(y >= low)
        def _(low=low):
            pieces = [ref.at[o] for ref, at in zip(sets, least) if at == low for o in range(ref.shape[0])]
            chunks = [(pieces[o : o + 2], None) for o in range(0, len(pieces), 2)]
            attend_all(QH if len(pieces) < NZ else QH // 2, q, chunks, state)

    if final:
        for h in range(QH):
            value = state[1][h, 0:HD, :] / state[1][h, HD : HD + 1, :]
            outs[0][:, HD * h : HD * h + HD] = jnp.transpose(value).astype(BF16)


def other_rows(place, q, sets, least, state, final=False):
    first = 2 + len(sets)
    head = (jax.ShapeDtypeStruct((TOK, QH * HD), BF16),) if final else ()
    return pl.pallas_call(
        functools.partial(rows_kernel, least, final),
        out_shape=head + STATE,
        in_specs=[SM] + [VM] * (3 + len(sets)),
        out_specs=[VM] * (len(head) + 2),
        input_output_aliases={first: len(head), first + 1: len(head) + 1},
        compiler_params=PARAMS,
        name="attend_final" if final else "attend_rows",
    )(place, q, *[in_hbm(a) for a in sets], *[in_vmem(a) for a in state])


def along_z(step):
    return [(y * NZ + z, y * NZ + (z + step) % NZ) for y in range(NY) for z in range(NZ)]


def along_y(pairs):
    return [(a * NZ + z, b * NZ + z) for a, b in pairs for z in range(NZ)]


def along_x(step):
    return [(x * NC + c, ((x + step) % NX) * NC + c) for x in range(NX) for c in range(NC)]


def per_device(
    ssm_inputs,
    state_maps,
    ssm_gates,
    time_steps,
    log_rates,
    skip_gain,
    conv_inputs,
    conv_maps,
    norm_gain,
    out_weight,
    queries,
    attention_keys,
    values,
):
    ctx = lax.axis_index("ctx")
    tp = lax.axis_index("tp")
    place = jnp.stack([tp % NC, tp // NC, ctx % NZ, ctx // NZ]).astype(jnp.int32)
    maps = state_maps.reshape(TOK, 256)
    taps_m = conv_maps.reshape(4, 256)

    edge, kv = prep(ssm_inputs, maps, attention_keys, values)
    halo = lax.ppermute(edge, "ctx", [(i, i + 1) for i in range(NY * NZ - 1)])
    f1 = lax.ppermute(kv, "ctx", along_z(1))
    b1 = lax.ppermute(kv, "ctx", along_z(-1))
    pack, xc, bc, cols, rows = local_part(
        halo, ssm_inputs, maps, conv_inputs, taps_m, time_steps, log_rates.reshape(1, HEADS)
    )
    f2 = lax.ppermute(f1, "ctx", along_z(1))
    b2 = lax.ppermute(b1, "ctx", along_z(-1))
    got = lax.all_to_all(pack, "ctx", 0, 0)
    f3 = lax.ppermute(f2, "ctx", along_z(1))
    b3 = lax.ppermute(b2, "ctx", along_z(-1))
    y0 = inner_part(skip_gain, xc, bc, cols, rows)
    f4 = lax.ppermute(f3, "ctx", along_z(1))
    scanned = scan_part(got)
    entering = lax.all_to_all(scanned, "ctx", 0, 0).reshape(CH, NS)

    pieces = [kv, f1, f2, f3, f4, b3, b2, b1]
    near, far = stack(pieces)
    up, down = along_y([(0, 1), (1, 2), (2, 3)]), along_y([(0, 3), (1, 0)])
    yfa = lax.ppermute(near, "ctx", up)
    yba = lax.ppermute(far, "ctx", down)
    state = own_row(place, queries, pieces, tuple(range(NZ)))
    y2f = lax.ppermute(yfa, "ctx", along_y([(1, 2), (2, 3)]))
    y2b = lax.ppermute(yba, "ctx", along_y([(3, 2), (0, 3)]))
    yfb = lax.ppermute(far, "ctx", up)
    ybb = lax.ppermute(near, "ctx", along_y([(0, 3)]))
    state = other_rows(place, queries, [yfa, yba], [1, 3], state)
    keep, send = project_part(
        place, y0, bc, entering, cols, ssm_gates, norm_gain.reshape(1, CH), out_weight
    )
    swapped = lax.ppermute(send, "tp", [(i, i ^ 1) for i in range(NX * NC)])
    sums = pair_sum(place, keep, swapped)
    others = []
    for s in range(1, NX):
        others.append(lax.ppermute(sums[s], "tp", along_x(s)))
    attn_out, *_ = other_rows(place, queries, [yfb, ybb, y2f, y2b], [1, 3, 2, 2], state, final=True)
    total = sums[0].astype(F32)
    for a in others:
        total = total + a.astype(F32)
    ssm_out = total.astype(BF16)
    return ssm_out, attn_out


def solution(mesh):
    placed = (
        P("ctx", "tp"),
        P("ctx", "tp", None),
        P("ctx", "tp"),
        P("tp", "ctx"),
        P("tp"),
        P("tp"),
        P(None, "tp"),
        P(None, "tp", None),
        P("tp"),
        P("tp", None),
        P("ctx", "tp"),
        P("ctx", "tp"),
        P("ctx", "tp"),
    )

    return jax.shard_map(
        per_device,
        mesh=mesh,
        in_specs=placed,
        out_specs=(P(("ctx", "tp"), None), P("ctx", "tp")),
        check_vma=False,
    )
```
